256 devices in a mesh: section: 8 (over z), expert: 32 (over x, y, core).
Axes of the slice: x: 4, y: 4, z: 8, core: 2. Of those that a mesh axis runs over, the one named last changes fastest.
Arguments:
- acts: bfloat16 [8, 8192, 2048], P('section', 'expert'), may hold values from -6 to 6
- expert_ids: int32 [8, 8192, 2], P('section', 'expert'), may hold values from 0 to 31, all different within a row; in each aligned block of 256 rows (0 to 255, 256 to 511, ..., all dimensions but the last counted through in order) at most 24 rows name the same one
- router: bfloat16 [8, 2048, 32], P('section'), may hold values from -0.125 to 0.125
- skip_gain: float32 [8, 2048], P('section'), may hold values from 0.5 to 1.5
- skip_rows: bfloat16 [8, 8192, 2048], P('section', 'expert'), may hold values from -6 to 6
- w_in: bfloat16 [8, 32, 2048, 1024], P('section', 'expert'), may hold values from -0.125 to 0.125
- w_out: bfloat16 [8, 32, 1024, 2048], P('section', 'expert'), may hold values from -0.1875 to 0.1875
Outputs:
- handed: bfloat16 [8, 8192, 2048], P('section', 'expert')
- mirrored: bfloat16 [8, 8192, 2048], P('section', 'expert')
The draws below stay inside these ranges and needn't reach their ends.
Inputs may be any that keep to these rules, and one draw needn't show every extreme that they name: `expert_ids`: each token names 2 different experts. Among the 256 tokens of one group no expert is named more than 24 times, a bound that some block reaches.
All inputs are finite; a program needn't handle non-finite values.
Results may differ from the reference program's by a relative error of at most 0.0041.
Values may be sent and summed in bfloat16 or wider, within the bound.
A program may use at most 64 MiB of HBM per device.

```python
import math
import jax
import jax.numpy as jnp
import numpy as np
from jax import lax

D = 2048
FF = 1024
TOP = 2
TOK_DEV = 256
EXPERTS = 32
TOKENS = 8192
SECTIONS = 8
CAP = 24
N_EXPERT = 32


def block_scale(key, extent, pieces, low, largest):
    factor_of = 1.0
    for axis_at, blocks in pieces:
        steps = jax.random.uniform(jax.random.fold_in(jax.random.fold_in(key, 6), axis_at), (blocks,), jnp.float32, low / len(pieces), largest / len(pieces))
        factor_of = factor_of * jnp.repeat(jnp.exp(steps), extent[axis_at] // blocks).reshape((-1,) + (1,) * (len(extent) - 1 - axis_at))
    return factor_of


def routed_block(stream_key, own, number, rows, number_of, top, bound, skew):
    sequence = jax.random.permutation(stream_key, number_of)
    heavy_load, usual = portions_of(number_of, rows * top, bound, skew, True), portions_of(number_of, rows * top, bound, skew, False)
    places = jnp.arange(number_of)

    def named(tallies, rotation):
        used = int((tallies > 0).sum())
        fixed = max(1, used // 4)
        shifted = fixed + (places - fixed + rotation * (used - fixed)) % max(1, number_of - fixed)
        return jnp.zeros((number_of,), jnp.int32).at[sequence[jnp.where(places < fixed, places, shifted)]].set(jnp.asarray(tallies, jnp.int32))

    tallies = jnp.where(number % 4 == 0, named(heavy_load, number // 4), named(usual, number - number // 4 - 1))
    mixed = jax.random.permutation(jax.random.fold_in(own, 3), number_of)
    source_of, sink = mixed[0:number_of // 2 * 2:2], mixed[1:number_of // 2 * 2:2]
    slack = jnp.minimum(tallies[source_of] - 1, bound - tallies[sink]) // 2
    slack = jnp.where((source_of == sequence[0]) | (sink == sequence[0]) | (tallies[sink] == 0), 0, jnp.maximum(slack, 0))
    shifted = jax.random.randint(jax.random.fold_in(own, 4), (number_of // 2,), 0, 1 << 20) % (slack + 1)
    tallies = tallies.at[source_of].add(-shifted).at[sink].add(shifted)
    items = jnp.searchsorted(jnp.cumsum(tallies), jnp.arange(rows * top), side="right").astype(jnp.int32)
    listing = items.reshape(top, rows).T
    listing = listing[jax.random.permutation(jax.random.fold_in(own, 1), rows)]
    rotation = jax.random.randint(jax.random.fold_in(own, 2), (rows, 1), 0, top)
    return jnp.take_along_axis(listing, (jnp.arange(top)[None, :] + rotation) % top, axis=1)


def portions_of(number_of, total, most, slope, full):
    portions = [(1 << 20) // math.isqrt(rank ** slope) + 1 for rank in range(1, number_of + 1)]
    largest = most if full else min(most, max(-(-total // number_of), total * portions[0] // sum(portions)))
    least = 1 if total - largest >= number_of - 1 else 0
    given, surplus = [largest] + [least] * (number_of - 1), total - largest - least * (number_of - 1)
    while surplus > 0:
        candidates = [i for i in range(1, number_of) if given[i] < largest] or [i for i in range(1, number_of) if given[i] < most]
        mass, left = sum([portions[i] for i in candidates]), surplus
        for i in candidates:
            extra = min(most - given[i], max(1, left * portions[i] // mass), surplus)
            given[i] = given[i] + extra
            surplus = surplus - extra
    return np.array(given)


def noise(key, dims, width, bound, shards=(), held_as=jnp.bfloat16):
    result = width * jax.random.normal(key, dims, jnp.float32)
    if shards:
        result = result * block_scale(key, dims, shards, -0.22, 0.18)
    return jnp.clip(result, -bound, bound).astype(held_as)


def setup_inputs(seed: int = 0) -> dict:
    seeds = jax.random.split(jax.random.key(seed), 8)
    acts = noise(seeds[0], (SECTIONS, TOKENS, D), 1.0, 6.0, ((0, 8), (1, 32)))
    expert_ids_keys = jax.random.split(jax.random.fold_in(seeds[1], 1), SECTIONS * TOKENS // TOK_DEV)
    expert_ids_turns = jax.random.permutation(jax.random.fold_in(seeds[1], 3), SECTIONS * TOKENS // TOK_DEV)
    expert_ids = jax.vmap(lambda own, number: routed_block(jax.random.fold_in(seeds[1], 2), own, number, TOK_DEV, EXPERTS, TOP, CAP, 2))(expert_ids_keys, expert_ids_turns).reshape((SECTIONS, TOKENS, TOP))
    router = noise(seeds[2], (SECTIONS, D, EXPERTS), D ** -0.5, 0.125, ((0, 8),))
    skip_gain = jnp.clip(0.5 + 1.0 * jax.random.uniform(seeds[3], (SECTIONS, D), jnp.float32) ** block_scale(seeds[3], (SECTIONS, D), ((0, 8),), -0.2, 0.2), 0.5, 1.5)
    skip_rows = noise(seeds[4], (SECTIONS, TOKENS, D), 1.0, 6.0, ((0, 8), (1, 32)))
    w_in = noise(seeds[5], (SECTIONS, EXPERTS, D, FF), D ** -0.5, 0.125, ((0, 8), (1, 32)))
    w_out = noise(seeds[6], (SECTIONS, EXPERTS, FF, D), FF ** -0.5, 0.1875, ((0, 8), (1, 32)))
    return dict(acts=acts, expert_ids=expert_ids, router=router, skip_gain=skip_gain, skip_rows=skip_rows, w_in=w_in, w_out=w_out)


def rms(values):
    return values * lax.rsqrt(lax.optimization_barrier(jnp.mean(values * values, axis=-1, keepdims=True)) + 1e-06)

def slots_of(group_ids):
    flat = group_ids.reshape(-1)
    onehot = (flat[:, None] == jnp.arange(EXPERTS, dtype=jnp.int32)[None, :]).astype(jnp.int32)
    before = jnp.cumsum(onehot, axis=0) - onehot
    return lax.optimization_barrier(jnp.sum(before * onehot, axis=1)).astype(jnp.int32).reshape(group_ids.shape)

def expert_apply(operands):
    rows, first, second = operands
    hidden = jax.nn.gelu(jnp.dot(rows, first, preferred_element_type=jnp.float32), approximate=True).astype(jnp.bfloat16)
    return jnp.dot(hidden, second, preferred_element_type=jnp.float32).astype(jnp.bfloat16)

def reference(acts, expert_ids, router, skip_gain, skip_rows, w_in, w_out):
    outputs = []
    for section in range(SECTIONS):
        h_rows = acts[section].astype(jnp.float32)
        if section >= SECTIONS // 2:
            h_rows = h_rows + skip_gain[section][None, :] * rms(skip_rows[section].astype(jnp.float32))
        normed = rms(h_rows).astype(jnp.bfloat16)
        logits = jnp.dot(normed, router[section], preferred_element_type=jnp.float32)
        chosen = jnp.take_along_axis(logits, expert_ids[section], axis=1)
        gates = jax.nn.softmax(chosen, axis=-1)
        groups = expert_ids[section].reshape(N_EXPERT, TOK_DEV, TOP)
        slot = jax.vmap(slots_of)(groups).reshape(TOKENS, TOP)
        source = (jnp.arange(TOKENS, dtype=jnp.int32) // TOK_DEV)[:, None]
        row_pos = (source * CAP + slot).reshape(-1).astype(jnp.int32)
        flat_ids = expert_ids[section].reshape(-1).astype(jnp.int32)
        repeated = jnp.repeat(normed, TOP, axis=0)
        buffer = jnp.zeros((EXPERTS, N_EXPERT * CAP, D), jnp.bfloat16).at[flat_ids, row_pos].set(repeated)
        expert_out = lax.map(expert_apply, (buffer, w_in[section], w_out[section]))
        fetched = expert_out[flat_ids, row_pos].reshape(TOKENS, TOP, D).astype(jnp.float32)
        combined = lax.optimization_barrier(jnp.sum(gates[:, :, None] * fetched, axis=1))
        outputs.append((h_rows + combined).astype(jnp.bfloat16))
    stacked = jnp.stack(outputs, axis=0)
    handed = jnp.roll(stacked, 1, axis=0)
    mirrored = stacked[::-1]
    return (handed, mirrored)
```

```python
import functools

import jax
import jax.numpy as jnp
from jax import lax
from jax.experimental import pallas as pl
from jax.experimental.pallas import tpu as pltpu
from jax.sharding import PartitionSpec as P

MESH = pl.DeviceIdType.MESH
F32 = jnp.float32
BF16 = jnp.bfloat16

IN_CHUNKS = 2
OUT_CHUNKS = 8


def rms(values):
    return values * lax.rsqrt(jnp.mean(values * values, axis=-1, keepdims=True) + 1e-06)


def iota(shape, axis):
    return lax.broadcasted_iota(jnp.int32, shape, axis)


def partner(sides, me, i):
    nx, ny, nc = sides
    x, y, core = me // (ny * nc), (me // nc) % ny, me % nc
    a, c, b = i % nx, (i // nx) % nc, i // (nx * nc)
    return ((x + a) % nx) * (ny * nc) + ((y + a + b) % ny) * nc + (core + c) % nc


def kernel(
    sides, sections, experts, cap,
    acts, ids, router, gain, skip, w_in, w_out,
    handed, mirrored,
    wi, wo, h, normed, place, mix, send, recv, rows, acc, hidden, outs, back, ys,
    w_sem, own_sem, in_send, in_recv, out_send, out_recv, z_send, z_recv, dup_sem,
):
    sec = lax.axis_index("section")
    me = lax.axis_index("expert")
    tok, width = acts.shape
    ff = w_in.shape[1]
    slots = experts * cap
    nxt, mir = (sec + 1) % sections, sections - 1 - sec
    prv = (sec + sections - 1) % sections

    copy_wi = pltpu.make_async_copy(w_in, wi, w_sem.at[0])
    copy_wo = pltpu.make_async_copy(w_out, wo, w_sem.at[1])
    copy_wi.start()
    copy_wo.start()

    barrier = pltpu.get_barrier_semaphore()

    def greet(i, carry):
        pl.semaphore_signal(barrier, inc=1, device_id=(sec, partner(sides, me, i)), device_id_type=MESH)
        return carry

    lax.fori_loop(1, experts, greet, 0)
    pl.semaphore_signal(barrier, inc=1, device_id=(prv, me), device_id_type=MESH)
    pl.semaphore_signal(barrier, inc=1, device_id=(mir, me), device_id_type=MESH)

    decoder = (sec >= sections // 2).astype(F32)
    block = 32

    def norm_rows(i, carry):
        at = pl.ds(pl.multiple_of(i * block, block), block)
        term = gain[...] * rms(skip[at, :].astype(F32))
        value = acts[at, :].astype(F32) + jnp.where(decoder > 0.5, term, jnp.zeros_like(term))
        h[at, :] = value
        normed[at, :] = rms(value).astype(BF16)
        return carry

    lax.fori_loop(0, tok // block, norm_rows, 0)

    id0, id1 = ids[0:1, :], ids[1:2, :]
    kinds = iota((experts, tok), 0)
    one0, one1 = (id0 == kinds).astype(F32), (id1 == kinds).astype(F32)
    earlier = (iota((tok, tok), 0) < iota((tok, tok), 1)).astype(F32).astype(BF16)
    before = jnp.dot((one0 + one1).astype(BF16), earlier, preferred_element_type=F32)
    slot0 = jnp.sum(before * one0, axis=0, keepdims=True)
    slot1 = jnp.sum(before * one1, axis=0, keepdims=True)
    row0 = id0 * cap + slot0.astype(jnp.int32)
    row1 = id1 * cap + slot1.astype(jnp.int32)
    spots = iota((slots, tok), 0)
    place[...] = jnp.logical_or(spots == row0, spots == row1).astype(F32).astype(BF16)

    in_width = width // IN_CHUNKS
    peers = 8

    def own_copy(c):
        return pltpu.make_async_copy(send.at[c, me], recv.at[c, me], in_recv.at[c])

    for c in range(IN_CHUNKS):
        def fill(i, carry, c=c):
            at = pl.ds(pl.multiple_of(i * peers * cap, peers * cap), peers * cap)
            got = jnp.dot(place[at, :], normed[:, c * in_width:(c + 1) * in_width], preferred_element_type=F32)
            send[c, pl.ds(i * peers, peers)] = got.reshape(peers, cap, in_width).astype(BF16)
            return carry

        lax.fori_loop(0, experts // peers, fill, 0)
        if c == 0:
            pl.semaphore_wait(barrier, experts + 1)

        def dispatch(i, carry, c=c):
            to = partner(sides, me, i)
            pltpu.make_async_remote_copy(
                src_ref=send.at[c, to], dst_ref=recv.at[c, me],
                send_sem=in_send.at[c], recv_sem=in_recv.at[c],
                device_id=(sec, to), device_id_type=MESH,
            ).start()
            return carry

        lax.fori_loop(1, experts, dispatch, 0)
        own_copy(c).start()

    logits = jnp.dot(normed[...], router[...], preferred_element_type=F32)
    lines = iota((8, tok), 0)
    info = jnp.where(lines == 0, id0.astype(F32), jnp.where(lines == 1, id1.astype(F32), jnp.where(lines == 2, slot0, slot1)))
    eye = (iota((tok, tok), 0) == iota((tok, tok), 1)).astype(F32).astype(BF16)
    column = lax.dot_general(eye, info.astype(BF16), (((1,), (1,)), ((), ())), preferred_element_type=F32)
    names = iota((tok, experts), 1).astype(F32)
    chosen0 = jnp.sum(jnp.where(names == column[:, 0:1], logits, 0.0), axis=1, keepdims=True)
    chosen1 = jnp.sum(jnp.where(names == column[:, 1:2], logits, 0.0), axis=1, keepdims=True)
    top = jnp.maximum(chosen0, chosen1)
    exp0, exp1 = jnp.exp(chosen0 - top), jnp.exp(chosen1 - top)
    gate0, gate1 = exp0 / (exp0 + exp1), exp1 / (exp0 + exp1)
    spot0 = column[:, 0:1] * cap + column[:, 2:3]
    spot1 = column[:, 1:2] * cap + column[:, 3:4]
    along = iota((tok, slots), 1).astype(F32)
    gates = jnp.where(along == spot0, gate0, 0.0) + jnp.where(along == spot1, gate1, 0.0)
    high = gates.astype(BF16)
    mix[0:tok, :] = high
    mix[tok:, :] = (gates - high.astype(F32)).astype(BF16)

    copy_wi.wait()
    pair = 2
    tile = 256
    for c in range(IN_CHUNKS):
        pltpu.make_async_copy(send.at[c], recv.at[c], in_recv.at[c]).wait()
        span = pl.ds(c * in_width, in_width)

        def flatten(i, carry, c=c, span=span):
            at = pl.ds(pl.multiple_of(i * pair * cap, pair * cap), pair * cap)
            got = recv[c, pl.ds(i * pair, pair)].astype(F32)
            rows[at, span] = got.reshape(pair * cap, in_width).astype(BF16)
            return carry

        lax.fori_loop(0, experts // pair, flatten, 0)

        def first(n, carry, c=c, span=span):
            at = pl.ds(pl.multiple_of(n * tile, tile), tile)
            got = jnp.dot(rows[:, span], wi[span, at], preferred_element_type=F32)
            if c > 0:
                got = acc[:, at] + got
            if c < IN_CHUNKS - 1:
                acc[:, at] = got
            else:
                hidden[:, at] = jax.nn.gelu(got, approximate=True).astype(BF16)
            return carry

        lax.fori_loop(0, ff // tile, first, 0)

    copy_wo.wait()
    out_width = width // OUT_CHUNKS

    def second(c, carry):
        at = pl.ds(pl.multiple_of(c * out_width, out_width), out_width)
        got = jnp.dot(hidden[...], wo[:, at], preferred_element_type=F32)
        outs[c] = got.reshape(experts, cap, out_width).astype(BF16)

        def give_back(i, inner):
            to = partner(sides, me, i)
            pltpu.make_async_remote_copy(
                src_ref=outs.at[c, to], dst_ref=back.at[c, me],
                send_sem=out_send.at[c], recv_sem=out_recv.at[c],
                device_id=(sec, to), device_id_type=MESH,
            ).start()
            return inner

        lax.fori_loop(1, experts, give_back, 0)
        pltpu.make_async_copy(outs.at[c, me], back.at[c, me], out_recv.at[c]).start()
        return carry

    lax.fori_loop(0, OUT_CHUNKS, second, 0)

    def to_next(c):
        at = pl.ds(pl.multiple_of(c * out_width, out_width), out_width)
        return pltpu.make_async_remote_copy(
            src_ref=ys.at[c], dst_ref=handed.at[:, at],
            send_sem=z_send.at[0, c], recv_sem=z_recv.at[0, c],
            device_id=(nxt, me), device_id_type=MESH,
        )

    def to_mirror(c):
        at = pl.ds(pl.multiple_of(c * out_width, out_width), out_width)
        return pltpu.make_async_remote_copy(
            src_ref=ys.at[c], dst_ref=mirrored.at[:, at],
            send_sem=z_send.at[1, c], recv_sem=z_recv.at[1, c],
            device_id=(mir, me), device_id_type=MESH,
        )

    def double(c):
        at = pl.ds(pl.multiple_of(c * out_width, out_width), out_width)
        return pltpu.make_async_copy(handed.at[:, at], mirrored.at[:, at], dup_sem.at[c])

    sends_one = nxt == mir
    gets_one = prv == mir

    def combine(c, carry):
        pltpu.make_async_copy(outs.at[c], back.at[c], out_recv.at[c]).wait()
        at = pl.ds(pl.multiple_of(c * out_width, out_width), out_width)
        got = back[c].astype(F32).reshape(slots, out_width).astype(BF16)
        both = jnp.dot(mix[...], got, preferred_element_type=F32)
        ys[c] = (h[:, at] + (both[0:tok] + both[tok:])).astype(BF16)
        to_next(c).start()

        @pl.when(jnp.logical_not(sends_one))
        def _():
            to_mirror(c).start()

        return carry

    lax.fori_loop(0, OUT_CHUNKS, combine, 0)

    def arrive(c, carry):
        to_next(c).wait_recv()

        @pl.when(gets_one)
        def _():
            double(c).start()

        @pl.when(jnp.logical_not(gets_one))
        def _():
            to_mirror(c).wait_recv()

        return carry

    lax.fori_loop(0, OUT_CHUNKS, arrive, 0)

    def finish(c, carry):
        @pl.when(gets_one)
        def _():
            double(c).wait()

        to_next(c).wait_send()

        @pl.when(jnp.logical_not(sends_one))
        def _():
            to_mirror(c).wait_send()

        others = pl.ds(0, experts - 1)
        pltpu.make_async_copy(outs.at[c, others], back.at[c, others], out_send.at[c]).wait()
        return carry

    lax.fori_loop(0, OUT_CHUNKS, finish, 0)
    for c in range(IN_CHUNKS):
        others = pl.ds(0, experts - 1)
        pltpu.make_async_copy(send.at[c, others], recv.at[c, others], in_send.at[c]).wait()


def local(sides, acts, expert_ids, router, skip_gain, skip_rows, w_in, w_out):
    sections = lax.axis_size("section")
    tok, width = acts.shape[1], acts.shape[2]
    experts = router.shape[2]
    topk = expert_ids.shape[2]
    cap = 3 * tok * topk // (2 * experts)
    ff = w_in.shape[3]
    slots = experts * cap
    in_width, out_width = width // IN_CHUNKS, width // OUT_CHUNKS
    vmem = pl.BlockSpec(memory_space=pltpu.VMEM)
    hbm = pl.BlockSpec(memory_space=pl.ANY)
    out = jax.ShapeDtypeStruct((tok, width), BF16)
    dma = pltpu.SemaphoreType.DMA
    handed, mirrored = pl.pallas_call(
        functools.partial(kernel, sides, sections, experts, cap),
        out_shape=(out, out),
        in_specs=[vmem, vmem, vmem, vmem, vmem, hbm, hbm],
        out_specs=(vmem, vmem),
        scratch_shapes=[
            pltpu.VMEM((width, ff), BF16),
            pltpu.VMEM((ff, width), BF16),
            pltpu.VMEM((tok, width), F32),
            pltpu.VMEM((tok, width), BF16),
            pltpu.VMEM((slots, tok), BF16),
            pltpu.VMEM((2 * tok, slots), BF16),
            pltpu.VMEM((IN_CHUNKS, experts, cap, in_width), BF16),
            pltpu.VMEM((IN_CHUNKS, experts, cap, in_width), BF16),
            pltpu.VMEM((slots, width), BF16),
            pltpu.VMEM((slots, ff), F32),
            pltpu.VMEM((slots, ff), BF16),
            pltpu.VMEM((OUT_CHUNKS, experts, cap, out_width), BF16),
            pltpu.VMEM((OUT_CHUNKS, experts, cap, out_width), BF16),
            pltpu.VMEM((OUT_CHUNKS, tok, out_width), BF16),
            dma((2,)),
            dma,
            dma((IN_CHUNKS,)),
            dma((IN_CHUNKS,)),
            dma((OUT_CHUNKS,)),
            dma((OUT_CHUNKS,)),
            dma((2, OUT_CHUNKS)),
            dma((2, OUT_CHUNKS)),
            dma((OUT_CHUNKS,)),
        ],
        compiler_params=pltpu.CompilerParams(
            collective_id=0, has_side_effects=True, vmem_limit_bytes=60 * 1024 * 1024
        ),
        name="moe_window",
    )(acts[0], expert_ids[0].T, router[0], skip_gain, skip_rows[0], w_in[0, 0], w_out[0, 0])
    return (handed[None], mirrored[None])


def solution(mesh):
    placed = (
        P("section", "expert", None),
        P("section", "expert", None),
        P("section", None, None),
        P("section", None),
        P("section", "expert", None),
        P("section", "expert", None, None),
        P("section", "expert", None, None),
    )
    return jax.shard_map(
        functools.partial(local, (4, 4, 2)),
        mesh=mesh,
        in_specs=placed,
        out_specs=(P("section", "expert", None), P("section", "expert", None)),
        check_vma=False,
    )
```

```python
import functools

import jax
import jax.numpy as jnp
from jax import lax
from jax.experimental import pallas as pl
from jax.experimental.pallas import tpu as pltpu
from jax.sharding import PartitionSpec as P

MESH = pl.DeviceIdType.MESH
F32 = jnp.float32
BF16 = jnp.bfloat16

IN_CHUNKS = 4
OUT_CHUNKS = 8
EARLY = 7
AFTER = (1, 3, 6)


def rms(values):
    return values * lax.rsqrt(jnp.mean(values * values, axis=-1, keepdims=True) + 1e-06)


def iota(shape, axis):
    return lax.broadcasted_iota(jnp.int32, shape, axis)


def partner(sides, chip, i):
    nx, ny = sides
    x, y, a, b = chip // ny, chip % ny, i % nx, i // nx
    return ((x + a) % nx) * ny + (y + a + b) % ny


def kernel(
    sides, sections, experts, cap,
    acts_in, ids_in, router_in, gain_in, skip_in, w_in, w_out,
    handed, mirrored,
    acts, ids, router, gain, skip, wi, wo, h, normed, place, mix, send, recv, rows, acc, hidden, outs, back, ys,
    w_sem, in_send, in_recv, out_send, out_recv, z_send, z_recv, dup_sem,
):
    sec = lax.axis_index("section")
    me = lax.axis_index("expert")
    core, chip = me % 2, me // 2
    chips = experts // 2
    first_core, second_core = core == 0, core == 1
    tok, width = acts.shape
    ff = w_in.shape[1]
    slots = experts * cap
    nxt, mir = (sec + 1) % sections, sections - 1 - sec
    prv = (sec + sections - 1) % sections

    loads = [
        pltpu.make_async_copy(source, target, w_sem.at[n])
        for n, (source, target) in enumerate((
            (acts_in, acts), (skip_in, skip), (gain_in, gain), (ids_in, ids),
            (router_in, router), (w_in, wi), (w_out, wo),
        ))
    ]
    for load in loads:
        load.start()
    copy_wi, copy_wo = loads[5], loads[6]

    barrier = pltpu.get_barrier_semaphore()

    def greet(i, carry):
        to = partner(sides, chip, i) * 2
        pl.semaphore_signal(barrier, inc=1, device_id=(sec, to), device_id_type=MESH)
        pl.semaphore_signal(barrier, inc=1, device_id=(sec, to + 1), device_id_type=MESH)
        return carry

    lax.fori_loop(1, chips, greet, 0)
    pl.semaphore_signal(barrier, inc=1, device_id=(sec, chip * 2 + 1 - core), device_id_type=MESH)
    pl.semaphore_signal(barrier, inc=1, device_id=(prv, me), device_id_type=MESH)
    pl.semaphore_signal(barrier, inc=1, device_id=(mir, me), device_id_type=MESH)

    for load in loads[0:3]:
        load.wait()
    decoder = (sec >= sections // 2).astype(F32)
    block = 32

    def norm_rows(i, carry):
        at = pl.ds(pl.multiple_of(i * block, block), block)
        term = gain[...] * rms(skip[at, :].astype(F32))
        value = acts[at, :].astype(F32) + jnp.where(decoder > 0.5, term, jnp.zeros_like(term))
        h[at, :] = value
        normed[at, :] = rms(value).astype(BF16)
        return carry

    lax.fori_loop(0, tok // block, norm_rows, 0)

    loads[3].wait()
    id0, id1 = ids[0:1, :], ids[1:2, :]
    kinds = iota((experts, tok), 0)
    one0, one1 = (id0 == kinds).astype(F32), (id1 == kinds).astype(F32)
    earlier = (iota((tok, tok), 0) < iota((tok, tok), 1)).astype(F32).astype(BF16)
    before = jnp.dot((one0 + one1).astype(BF16), earlier, preferred_element_type=F32)
    slot0 = jnp.sum(before * one0, axis=0, keepdims=True)
    slot1 = jnp.sum(before * one1, axis=0, keepdims=True)
    row0 = id0 * cap + slot0.astype(jnp.int32)
    row1 = id1 * cap + slot1.astype(jnp.int32)
    spots = iota((slots, tok), 0)
    place[...] = jnp.logical_or(spots == row0, spots == row1).astype(F32).astype(BF16)

    in_width = width // IN_CHUNKS
    peers = 8

    def dispatch(c):
        def to_core(to):
            pltpu.make_async_remote_copy(
                src_ref=send.at[c, to], dst_ref=recv.at[core, c, chip],
                send_sem=in_send.at[c], recv_sem=in_recv.at[core, c],
                device_id=(sec, to), device_id_type=MESH,
            ).start()

        def to_chip(i, carry):
            to = partner(sides, chip, i) * 2
            to_core(to + 1 - core)
            to_core(to + core)
            return carry

        lax.fori_loop(1, chips, to_chip, 0)
        to_core(chip * 2 + 1 - core)
        pltpu.make_async_copy(send.at[c, me], recv.at[core, c, chip], in_recv.at[core, c]).start()

    for c in range(IN_CHUNKS):
        def fill(i, carry, c=c):
            at = pl.ds(pl.multiple_of(i * peers * cap, peers * cap), peers * cap)
            got = jnp.dot(place[at, :], normed[:, c * in_width:(c + 1) * in_width], preferred_element_type=F32)
            send[c, pl.ds(i * peers, peers)] = got.reshape(peers, cap, in_width).astype(BF16)
            return carry

        lax.fori_loop(0, experts // peers, fill, 0)
        if c == 0:
            pl.semaphore_wait(barrier, experts + 1)

        @pl.when(first_core)
        def _(c=c):
            dispatch(c)

    loads[4].wait()
    logits = lax.dot_general(normed[...], router[...], (((1,), (1,)), ((), ())), preferred_element_type=F32)
    lines = iota((8, tok), 0)
    info = jnp.where(lines == 0, id0.astype(F32), jnp.where(lines == 1, id1.astype(F32), jnp.where(lines == 2, slot0, slot1)))
    eye = (iota((tok, tok), 0) == iota((tok, tok), 1)).astype(F32).astype(BF16)
    column = lax.dot_general(eye, info.astype(BF16), (((1,), (1,)), ((), ())), preferred_element_type=F32)
    names = iota((tok, experts), 1).astype(F32)
    chosen0 = jnp.sum(jnp.where(names == column[:, 0:1], logits, 0.0), axis=1, keepdims=True)
    chosen1 = jnp.sum(jnp.where(names == column[:, 1:2], logits, 0.0), axis=1, keepdims=True)
    top = jnp.maximum(chosen0, chosen1)
    exp0, exp1 = jnp.exp(chosen0 - top), jnp.exp(chosen1 - top)
    gate0, gate1 = exp0 / (exp0 + exp1), exp1 / (exp0 + exp1)
    spot0 = column[:, 0:1] * cap + column[:, 2:3]
    spot1 = column[:, 1:2] * cap + column[:, 3:4]
    along = iota((tok, slots), 1).astype(F32)
    gates = jnp.where(along == spot0, gate0, 0.0) + jnp.where(along == spot1, gate1, 0.0)
    high = gates.astype(BF16)
    mix[0:tok, :] = high
    mix[tok:, :] = (gates - high.astype(F32)).astype(BF16)

    copy_wi.wait()
    pair = 2
    tile = 256

    def enter(group):
        for c in range(IN_CHUNKS):
            pltpu.make_async_copy(recv.at[group, c], recv.at[group, c], in_recv.at[group, c]).wait()
            if group == 0 and c == IN_CHUNKS - 1:
                @pl.when(second_core)
                def _():
                    dispatch(0)

            span = pl.ds(c * in_width, in_width)

            def flatten(i, carry, c=c, span=span):
                at = pl.ds(pl.multiple_of(i * pair * cap, pair * cap), pair * cap)
                got = recv[group, c, pl.ds(i * pair, pair)].astype(F32)
                rows[at, span] = got.reshape(pair * cap, in_width).astype(BF16)
                return carry

            lax.fori_loop(0, chips // pair, flatten, 0)

            def first(n, carry, c=c, span=span):
                at = pl.ds(pl.multiple_of(n * tile, tile), tile)
                got = jnp.dot(rows[:, span], wi[span, at], preferred_element_type=F32)
                if c > 0:
                    got = acc[:, at] + got
                if c < IN_CHUNKS - 1:
                    acc[:, at] = got
                else:
                    hidden[:, at] = jax.nn.gelu(got, approximate=True).astype(BF16)
                return carry

            lax.fori_loop(0, ff // tile, first, 0)

    out_width = width // OUT_CHUNKS

    def leave(group, c):
        at = pl.ds(pl.multiple_of(c * out_width, out_width), out_width)
        got = jnp.dot(hidden[...], wo[:, at], preferred_element_type=F32)
        outs[group, c] = got.reshape(chips, cap, out_width).astype(BF16)

        def give_back(to):
            pltpu.make_async_remote_copy(
                src_ref=outs.at[group, c, to], dst_ref=back.at[c, me],
                send_sem=out_send.at[group, c], recv_sem=out_recv.at[c],
                device_id=(sec, to * 2 + group), device_id_type=MESH,
            ).start()

        def to_chip(i, carry):
            give_back(partner(sides, chip, i))
            return carry

        lax.fori_loop(1, chips, to_chip, 0)

        @pl.when(core == group)
        def _():
            pltpu.make_async_copy(outs.at[group, c, chip], back.at[c, me], out_recv.at[c]).start()

        @pl.when(core != group)
        def _():
            give_back(chip)

    def to_next(c):
        at = pl.ds(pl.multiple_of(c * out_width, out_width), out_width)
        return pltpu.make_async_remote_copy(
            src_ref=ys.at[c], dst_ref=handed.at[:, at],
            send_sem=z_send.at[0, c], recv_sem=z_recv.at[0, c],
            device_id=(nxt, me), device_id_type=MESH,
        )

    def to_mirror(c):
        at = pl.ds(pl.multiple_of(c * out_width, out_width), out_width)
        return pltpu.make_async_remote_copy(
            src_ref=ys.at[c], dst_ref=mirrored.at[:, at],
            send_sem=z_send.at[1, c], recv_sem=z_recv.at[1, c],
            device_id=(mir, me), device_id_type=MESH,
        )

    def double(c):
        at = pl.ds(pl.multiple_of(c * out_width, out_width), out_width)
        return pltpu.make_async_copy(handed.at[:, at], mirrored.at[:, at], dup_sem.at[c])

    sends_one = nxt == mir
    gets_one = prv == mir

    def combine(c, carry):
        pltpu.make_async_copy(back.at[c], back.at[c], out_recv.at[c]).wait()
        at = pl.ds(pl.multiple_of(c * out_width, out_width), out_width)
        got = back[c].astype(F32).reshape(slots, out_width).astype(BF16)
        both = jnp.dot(mix[...], got, preferred_element_type=F32)
        ys[c] = (h[:, at] + (both[0:tok] + both[tok:])).astype(BF16)
        to_next(c).start()

        @pl.when(jnp.logical_not(sends_one))
        def _():
            to_mirror(c).start()

        return carry

    enter(0)
    copy_wo.wait()

    def leave_first(c, carry):
        leave(0, c)
        for part, after in enumerate(AFTER):
            @pl.when(jnp.logical_and(second_core, c == after))
            def _(part=part):
                dispatch(part + 1)

        return carry

    lax.fori_loop(0, OUT_CHUNKS, leave_first, 0)

    @pl.when(first_core)
    def _():
        lax.fori_loop(0, EARLY, combine, 0)

    enter(1)

    def leave_second(c, carry):
        leave(1, c)
        return carry

    lax.fori_loop(0, OUT_CHUNKS, leave_second, 0)
    lax.fori_loop(jnp.where(first_core, EARLY, 0), OUT_CHUNKS, combine, 0)

    def arrive(c, carry):
        to_next(c).wait_recv()

        @pl.when(gets_one)
        def _():
            double(c).start()

        @pl.when(jnp.logical_not(gets_one))
        def _():
            to_mirror(c).wait_recv()

        return carry

    lax.fori_loop(0, OUT_CHUNKS, arrive, 0)

    def sent(group, c, count):
        some = pl.ds(0, count)
        pltpu.make_async_copy(outs.at[group, c, some], outs.at[group, c, some], out_send.at[group, c]).wait()

    def finish(c, carry):
        @pl.when(gets_one)
        def _():
            double(c).wait()

        to_next(c).wait_send()

        @pl.when(jnp.logical_not(sends_one))
        def _():
            to_mirror(c).wait_send()

        @pl.when(first_core)
        def _():
            sent(0, c, chips - 1)
            sent(1, c, chips)

        @pl.when(second_core)
        def _():
            sent(0, c, chips)
            sent(1, c, chips - 1)

        return carry

    lax.fori_loop(0, OUT_CHUNKS, finish, 0)
    for c in range(IN_CHUNKS):
        others = pl.ds(0, experts - 1)
        pltpu.make_async_copy(send.at[c, others], send.at[c, others], in_send.at[c]).wait()


def local(sides, acts, expert_ids, router, skip_gain, skip_rows, w_in, w_out):
    sections = lax.axis_size("section")
    tok, width = acts.shape[1], acts.shape[2]
    experts = router.shape[2]
    topk = expert_ids.shape[2]
    cap = 3 * tok * topk // (2 * experts)
    ff = w_in.shape[3]
    slots = experts * cap
    in_width, out_width = width // IN_CHUNKS, width // OUT_CHUNKS
    vmem = pl.BlockSpec(memory_space=pltpu.VMEM)
    hbm = pl.BlockSpec(memory_space=pltpu.HBM)
    out = jax.ShapeDtypeStruct((tok, width), BF16)
    dma = pltpu.SemaphoreType.DMA
    handed, mirrored = pl.pallas_call(
        functools.partial(kernel, sides, sections, experts, cap),
        out_shape=(out, out),
        in_specs=[hbm] * 7,
        out_specs=(vmem, vmem),
        scratch_shapes=[
            pltpu.VMEM((tok, width), BF16),
            pltpu.VMEM((topk, tok), jnp.int32),
            pltpu.VMEM((experts, width), BF16),
            pltpu.VMEM((1, width), F32),
            pltpu.VMEM((tok, width), BF16),
            pltpu.VMEM((width, ff), BF16),
            pltpu.VMEM((ff, width), BF16),
            pltpu.VMEM((tok, width), F32),
            pltpu.VMEM((tok, width), BF16),
            pltpu.VMEM((slots, tok), BF16),
            pltpu.VMEM((2 * tok, slots), BF16),
            pltpu.VMEM((IN_CHUNKS, experts, cap, in_width), BF16),
            pltpu.VMEM((2, IN_CHUNKS, experts // 2, cap, in_width), BF16),
            pltpu.VMEM((slots // 2, width), BF16),
            pltpu.VMEM((slots // 2, ff), F32),
            pltpu.VMEM((slots // 2, ff), BF16),
            pltpu.VMEM((2, OUT_CHUNKS, experts // 2, cap, out_width), BF16),
            pltpu.VMEM((OUT_CHUNKS, experts, cap, out_width), BF16),
            pltpu.VMEM((OUT_CHUNKS, tok, out_width), BF16),
            dma((7,)),
            dma((IN_CHUNKS,)),
            dma((2, IN_CHUNKS)),
            dma((2, OUT_CHUNKS)),
            dma((OUT_CHUNKS,)),
            dma((2, OUT_CHUNKS)),
            dma((2, OUT_CHUNKS)),
            dma((OUT_CHUNKS,)),
        ],
        compiler_params=pltpu.CompilerParams(
            collective_id=0, has_side_effects=True, vmem_limit_bytes=44 * 1024 * 1024
        ),
        name="moe_window",
    )(*(
        pltpu.with_memory_space_constraint(value, pltpu.HBM)
        for value in (acts[0], expert_ids[0].T, router[0].T, skip_gain, skip_rows[0], w_in[0, 0], w_out[0, 0])
    ))
    return (handed[None], mirrored[None])


def solution(mesh):
    placed = (
        P("section", "expert", None),
        P("section", "expert", None),
        P("section", None, None),
        P("section", None),
        P("section", "expert", None),
        P("section", "expert", None, None),
        P("section", "expert", None, None),
    )
    return jax.shard_map(
        functools.partial(local, (4, 4)),
        mesh=mesh,
        in_specs=placed,
        out_specs=(P("section", "expert", None), P("section", "expert", None)),
        check_vma=False,
    )
```

```python
import functools

import jax
import jax.numpy as jnp
from jax import lax
from jax.experimental import pallas as pl
from jax.experimental.pallas import tpu as pltpu
from jax.sharding import PartitionSpec as P

MESH = pl.DeviceIdType.MESH
F32 = jnp.float32
BF16 = jnp.bfloat16

IN_CHUNKS = 4
OUT_CHUNKS = 8
EARLY = 6
AFTER = (1, 3, 5)
LEAD = 2
GAP = 2


def rms(values):
    return values * lax.rsqrt(jnp.mean(values * values, axis=-1, keepdims=True) + 1e-06)


def iota(shape, axis):
    return lax.broadcasted_iota(jnp.int32, shape, axis)


def partners(sides, chip):
    nx, ny = sides
    x, y = chip // ny, chip % ny
    columns = [(x + a) % nx * ny for a in range(nx)]
    lines = [(y + b) % ny for b in range(ny)]
    return [columns[a] + lines[(a + b) % ny] for b in range(ny) for a in range(nx)]


def kernel(
    sides, sections, experts, cap,
    acts_in, ids_in, router_in, gain_in, skip_in, w_in, w_out,
    handed, mirrored,
    acts, ids, router, gain, skip, wi, wo, h, normed, place, mix, send, recv, rows, acc, hidden, outs, back, ys,
    w_sem, in_send, in_recv, out_send, out_recv, z_send, z_recv, dup_sem,
):
    sec = lax.axis_index("section")
    me = lax.axis_index("expert")
    core, chip = me % 2, me // 2
    chips = experts // 2
    first_core, second_core = core == 0, core == 1
    tok, width = acts.shape
    ff = w_in.shape[1]
    slots = experts * cap
    nxt, mir = (sec + 1) % sections, sections - 1 - sec
    prv = (sec + sections - 1) % sections

    loads = [
        pltpu.make_async_copy(source, target, w_sem.at[n])
        for n, (source, target) in enumerate((
            (acts_in, acts), (skip_in, skip), (gain_in, gain), (ids_in, ids),
            (router_in, router), (w_in, wi), (w_out, wo),
        ))
    ]
    for n in (3, 0, 1, 2, 4):
        loads[n].start()
    copy_wi, copy_wo = loads[5], loads[6]

    barrier = pltpu.get_barrier_semaphore()

    around = partners(sides, chip)
    for place_of in around[1:]:
        for side in (0, 1):
            pl.semaphore_signal(barrier, inc=1, device_id=(sec, place_of * 2 + side), device_id_type=MESH)
    pl.semaphore_signal(barrier, inc=1, device_id=(sec, chip * 2 + 1 - core), device_id_type=MESH)
    pl.semaphore_signal(barrier, inc=1, device_id=(prv, me), device_id_type=MESH)
    pl.semaphore_signal(barrier, inc=1, device_id=(mir, me), device_id_type=MESH)

    loads[3].wait()
    id0, id1 = ids[0:1, :], ids[1:2, :]
    kinds = iota((experts, tok), 0)
    one0, one1 = (id0 == kinds).astype(F32), (id1 == kinds).astype(F32)
    earlier = (iota((tok, tok), 0) < iota((tok, tok), 1)).astype(F32).astype(BF16)
    before = jnp.dot((one0 + one1).astype(BF16), earlier, preferred_element_type=F32)
    slot0 = jnp.sum(before * one0, axis=0, keepdims=True)
    slot1 = jnp.sum(before * one1, axis=0, keepdims=True)
    row0 = id0 * cap + slot0.astype(jnp.int32)
    row1 = id1 * cap + slot1.astype(jnp.int32)
    spots = iota((slots, tok), 0)
    place[...] = jnp.logical_or(spots == row0, spots == row1).astype(F32).astype(BF16)

    for load in loads[0:3]:
        load.wait()
    copy_wi.start()
    copy_wo.start()
    decoder = (sec >= sections // 2).astype(F32)
    block = 32

    def norm_rows(i, carry):
        at = pl.ds(pl.multiple_of(i * block, block), block)
        term = gain[...] * rms(skip[at, :].astype(F32))
        value = acts[at, :].astype(F32) + jnp.where(decoder > 0.5, term, jnp.zeros_like(term))
        h[at, :] = value
        normed[at, :] = rms(value).astype(BF16)
        return carry

    lax.fori_loop(0, tok // block, norm_rows, 0)

    in_width = width // IN_CHUNKS
    peers = 8

    def dispatch(c):
        def to_core(to):
            pltpu.make_async_remote_copy(
                src_ref=send.at[c, to], dst_ref=recv.at[core, c, chip],
                send_sem=in_send.at[c], recv_sem=in_recv.at[core, c],
                device_id=(sec, to), device_id_type=MESH,
            ).start()

        for place_of in around[1:]:
            to_core(place_of * 2 + 1 - core)
            to_core(place_of * 2 + core)
        to_core(chip * 2 + 1 - core)
        pltpu.make_async_copy(send.at[c, me], recv.at[core, c, chip], in_recv.at[core, c]).start()

    for c in range(IN_CHUNKS):
        def fill(i, carry, c=c):
            at = pl.ds(pl.multiple_of(i * peers * cap, peers * cap), peers * cap)
            got = jnp.dot(place[at, :], normed[:, c * in_width:(c + 1) * in_width], preferred_element_type=F32)
            send[c, pl.ds(i * peers, peers)] = got.reshape(peers, cap, in_width).astype(BF16)
            return carry

        lax.fori_loop(0, experts // peers, fill, 0)
        if c == 0:
            pl.semaphore_wait(barrier, experts + 1)

        @pl.when(first_core)
        def _(c=c):
            dispatch(c)

    loads[4].wait()
    logits = lax.dot_general(normed[...], router[...], (((1,), (1,)), ((), ())), preferred_element_type=F32)
    lines = iota((8, tok), 0)
    info = jnp.where(lines == 0, id0.astype(F32), jnp.where(lines == 1, id1.astype(F32), jnp.where(lines == 2, slot0, slot1)))
    eye = (iota((tok, tok), 0) == iota((tok, tok), 1)).astype(F32).astype(BF16)
    column = lax.dot_general(eye, info.astype(BF16), (((1,), (1,)), ((), ())), preferred_element_type=F32)
    names = iota((tok, experts), 1).astype(F32)
    chosen0 = jnp.sum(jnp.where(names == column[:, 0:1], logits, 0.0), axis=1, keepdims=True)
    chosen1 = jnp.sum(jnp.where(names == column[:, 1:2], logits, 0.0), axis=1, keepdims=True)
    top = jnp.maximum(chosen0, chosen1)
    exp0, exp1 = jnp.exp(chosen0 - top), jnp.exp(chosen1 - top)
    gate0, gate1 = exp0 / (exp0 + exp1), exp1 / (exp0 + exp1)
    spot0 = column[:, 0:1] * cap + column[:, 2:3]
    spot1 = column[:, 1:2] * cap + column[:, 3:4]
    along = iota((tok, slots), 1).astype(F32)
    gates = jnp.where(along == spot0, gate0, 0.0) + jnp.where(along == spot1, gate1, 0.0)
    high = gates.astype(BF16)
    mix[0:tok, :] = high
    mix[tok:, :] = (gates - high.astype(F32)).astype(BF16)

    copy_wi.wait()
    pair = 2
    tile = 256

    def enter(group):
        for c in range(IN_CHUNKS):
            pltpu.make_async_copy(recv.at[group, c], recv.at[group, c], in_recv.at[group, c]).wait()
            if group == 0 and c == IN_CHUNKS - 1:
                @pl.when(second_core)
                def _():
                    dispatch(0)

            span = pl.ds(c * in_width, in_width)

            def flatten(i, carry, c=c, span=span):
                at = pl.ds(pl.multiple_of(i * pair * cap, pair * cap), pair * cap)
                got = recv[group, c, pl.ds(i * pair, pair)].astype(F32)
                rows[at, span] = got.reshape(pair * cap, in_width).astype(BF16)
                return carry

            lax.fori_loop(0, chips // pair, flatten, 0)

            def first(n, carry, c=c, span=span):
                at = pl.ds(pl.multiple_of(n * tile, tile), tile)
                got = jnp.dot(rows[:, span], wi[span, at], preferred_element_type=F32)
                if c > 0:
                    got = acc[:, at] + got
                if c < IN_CHUNKS - 1:
                    acc[:, at] = got
                else:
                    hidden[:, at] = jax.nn.gelu(got, approximate=True).astype(BF16)
                return carry

            lax.fori_loop(0, ff // tile, first, 0)

    out_width = width // OUT_CHUNKS

    def leave(group, c):
        at = pl.ds(pl.multiple_of(c * out_width, out_width), out_width)
        got = jnp.dot(hidden[...], wo[:, at], preferred_element_type=F32)
        outs[group, c] = got.reshape(chips, cap, out_width).astype(BF16)

        def give_back(to):
            pltpu.make_async_remote_copy(
                src_ref=outs.at[group, c, to], dst_ref=back.at[c, me],
                send_sem=out_send.at[group, c], recv_sem=out_recv.at[c],
                device_id=(sec, to * 2 + group), device_id_type=MESH,
            ).start()

        for place_of in around[1:]:
            give_back(place_of)

        @pl.when(core == group)
        def _():
            pltpu.make_async_copy(outs.at[group, c, chip], back.at[c, me], out_recv.at[c]).start()

        @pl.when(core != group)
        def _():
            give_back(chip)

    def to_next(c):
        at = pl.ds(pl.multiple_of(c * out_width, out_width), out_width)
        return pltpu.make_async_remote_copy(
            src_ref=ys.at[c], dst_ref=handed.at[:, at],
            send_sem=z_send.at[0, c], recv_sem=z_recv.at[0, c],
            device_id=(nxt, me), device_id_type=MESH,
        )

    def to_mirror(c):
        at = pl.ds(pl.multiple_of(c * out_width, out_width), out_width)
        return pltpu.make_async_remote_copy(
            src_ref=ys.at[c], dst_ref=mirrored.at[:, at],
            send_sem=z_send.at[1, c], recv_sem=z_recv.at[1, c],
            device_id=(mir, me), device_id_type=MESH,
        )

    def double(c):
        at = pl.ds(pl.multiple_of(c * out_width, out_width), out_width)
        return pltpu.make_async_copy(handed.at[:, at], mirrored.at[:, at], dup_sem.at[c])

    sends_one = nxt == mir
    gets_one = prv == mir

    def combine(c, carry):
        pltpu.make_async_copy(back.at[c], back.at[c], out_recv.at[c]).wait()
        at = pl.ds(pl.multiple_of(c * out_width, out_width), out_width)
        got = back[c].astype(F32).reshape(slots, out_width).astype(BF16)
        both = jnp.dot(mix[...], got, preferred_element_type=F32)
        ys[c] = (h[:, at] + (both[0:tok] + both[tok:])).astype(BF16)
        to_next(c).start()

        @pl.when(jnp.logical_not(sends_one))
        def _():
            to_mirror(c).start()

        return carry

    enter(0)
    copy_wo.wait()

    def begin(j, carry):
        @pl.when(j < OUT_CHUNKS)
        def _():
            leave(0, j)

        for part, after in enumerate(AFTER):
            @pl.when(jnp.logical_and(second_core, j == after))
            def _(part=part):
                dispatch(part + 1)

        c = j - GAP

        @pl.when(jnp.logical_and(first_core, jnp.logical_and(c >= 0, c < EARLY)))
        def _():
            combine(c, 0)

        return carry

    lax.fori_loop(0, max(OUT_CHUNKS, EARLY + GAP), begin, 0)
    enter(1)

    def last(j, carry):
        @pl.when(j < OUT_CHUNKS)
        def _():
            leave(1, j)

        c = j + jnp.where(first_core, EARLY, -LEAD)

        @pl.when(jnp.logical_and(c >= 0, c < OUT_CHUNKS))
        def _():
            combine(c, 0)

        return carry

    lax.fori_loop(0, OUT_CHUNKS + LEAD, last, 0)

    def arrive(c, carry):
        to_next(c).wait_recv()

        @pl.when(gets_one)
        def _():
            double(c).start()

        @pl.when(jnp.logical_not(gets_one))
        def _():
            to_mirror(c).wait_recv()

        return carry

    lax.fori_loop(0, OUT_CHUNKS, arrive, 0)

    def sent(group, c, count):
        some = pl.ds(0, count)
        pltpu.make_async_copy(outs.at[group, c, some], outs.at[group, c, some], out_send.at[group, c]).wait()

    def finish(c, carry):
        @pl.when(gets_one)
        def _():
            double(c).wait()

        to_next(c).wait_send()

        @pl.when(jnp.logical_not(sends_one))
        def _():
            to_mirror(c).wait_send()

        @pl.when(first_core)
        def _():
            sent(0, c, chips - 1)
            sent(1, c, chips)

        @pl.when(second_core)
        def _():
            sent(0, c, chips)
            sent(1, c, chips - 1)

        return carry

    lax.fori_loop(0, OUT_CHUNKS, finish, 0)
    for c in range(IN_CHUNKS):
        others = pl.ds(0, experts - 1)
        pltpu.make_async_copy(send.at[c, others], send.at[c, others], in_send.at[c]).wait()


def local(sides, acts, expert_ids, router, skip_gain, skip_rows, w_in, w_out):
    sections = lax.axis_size("section")
    tok, width = acts.shape[1], acts.shape[2]
    experts = router.shape[2]
    topk = expert_ids.shape[2]
    cap = 3 * tok * topk // (2 * experts)
    ff = w_in.shape[3]
    slots = experts * cap
    in_width, out_width = width // IN_CHUNKS, width // OUT_CHUNKS
    vmem = pl.BlockSpec(memory_space=pltpu.VMEM)
    hbm = pl.BlockSpec(memory_space=pltpu.HBM)
    out = jax.ShapeDtypeStruct((tok, width), BF16)
    dma = pltpu.SemaphoreType.DMA
    handed, mirrored = pl.pallas_call(
        functools.partial(kernel, sides, sections, experts, cap),
        out_shape=(out, out),
        in_specs=[hbm] * 7,
        out_specs=(vmem, vmem),
        scratch_shapes=[
            pltpu.VMEM((tok, width), BF16),
            pltpu.VMEM((topk, tok), jnp.int32),
            pltpu.VMEM((experts, width), BF16),
            pltpu.VMEM((1, width), F32),
            pltpu.VMEM((tok, width), BF16),
            pltpu.VMEM((width, ff), BF16),
            pltpu.VMEM((ff, width), BF16),
            pltpu.VMEM((tok, width), F32),
            pltpu.VMEM((tok, width), BF16),
            pltpu.VMEM((slots, tok), BF16),
            pltpu.VMEM((2 * tok, slots), BF16),
            pltpu.VMEM((IN_CHUNKS, experts, cap, in_width), BF16),
            pltpu.VMEM((2, IN_CHUNKS, experts // 2, cap, in_width), BF16),
            pltpu.VMEM((slots // 2, width), BF16),
            pltpu.VMEM((slots // 2, ff), F32),
            pltpu.VMEM((slots // 2, ff), BF16),
            pltpu.VMEM((2, OUT_CHUNKS, experts // 2, cap, out_width), BF16),
            pltpu.VMEM((OUT_CHUNKS, experts, cap, out_width), BF16),
            pltpu.VMEM((OUT_CHUNKS, tok, out_width), BF16),
            dma((7,)),
            dma((IN_CHUNKS,)),
            dma((2, IN_CHUNKS)),
            dma((2, OUT_CHUNKS)),
            dma((OUT_CHUNKS,)),
            dma((2, OUT_CHUNKS)),
            dma((2, OUT_CHUNKS)),
            dma((OUT_CHUNKS,)),
        ],
        compiler_params=pltpu.CompilerParams(
            collective_id=0, has_side_effects=True, vmem_limit_bytes=44 * 1024 * 1024
        ),
        name="moe_window",
    )(*(
        pltpu.with_memory_space_constraint(value, pltpu.HBM)
        for value in (acts[0], expert_ids[0].T, router[0].T, skip_gain, skip_rows[0], w_in[0, 0], w_out[0, 0])
    ))
    return (handed[None], mirrored[None])


def solution(mesh):
    placed = (
        P("section", "expert", None),
        P("section", "expert", None),
        P("section", None, None),
        P("section", None),
        P("section", "expert", None),
        P("section", "expert", None, None),
        P("section", "expert", None, None),
    )
    return jax.shard_map(
        functools.partial(local, (4, 4)),
        mesh=mesh,
        in_specs=placed,
        out_specs=(P("section", "expert", None), P("section", "expert", None)),
        check_vma=False,
    )
```

```python
import functools

import jax
import jax.numpy as jnp
from jax import lax
from jax.experimental import pallas as pl
from jax.experimental.pallas import tpu as pltpu
from jax.sharding import PartitionSpec as P

MESH = pl.DeviceIdType.MESH
F32 = jnp.float32
BF16 = jnp.bfloat16

IN_CHUNKS = 4
OUT_CHUNKS = 8
EARLY = 6
AFTER = (1, 3, 5)
LEAD = 2
GAP = 2


def rms(values):
    return values * lax.rsqrt(jnp.mean(values * values, axis=-1, keepdims=True) + 1e-06)


def iota(shape, axis):
    return lax.broadcasted_iota(jnp.int32, shape, axis)


def partners(sides, chip):
    nx, ny = sides
    x, y = chip // ny, chip % ny
    columns = [(x + a) % nx * ny for a in range(nx)]
    lines = [(y + b) % ny for b in range(ny)]
    steps = [(a, (a + b) % ny) for b in range(ny) for a in range(nx)]
    reach = lambda step: min(step[0], nx - step[0]) + min(step[1], ny - step[1])
    return [columns[a] + lines[b] for a, b in steps[:1] + sorted(steps[1:], key=reach, reverse=True)]


def kernel(
    sides, sections, experts, cap,
    acts_in, ids_in, router_in, gain_in, skip_in, w_in, w_out,
    handed, mirrored,
    acts, ids, router, gain, skip, wi, wo, h, normed, place, mix, send, recv, rows, acc, hidden, outs, back, ys,
    w_sem, in_send, in_recv, out_send, out_recv, z_send, z_recv, dup_sem,
):
    sec = lax.axis_index("section")
    me = lax.axis_index("expert")
    core, chip = me % 2, me // 2
    chips = experts // 2
    first_core, second_core = core == 0, core == 1
    tok, width = acts.shape
    ff = w_in.shape[1]
    slots = experts * cap
    nxt, mir = (sec + 1) % sections, sections - 1 - sec
    prv = (sec + sections - 1) % sections

    loads = [
        pltpu.make_async_copy(source, target, w_sem.at[n])
        for n, (source, target) in enumerate((
            (acts_in, acts), (skip_in, skip), (gain_in, gain), (ids_in, ids),
            (router_in, router), (w_in, wi), (w_out, wo),
        ))
    ]
    for n in (3, 0, 1, 2, 4):
        loads[n].start()
    copy_wi, copy_wo = loads[5], loads[6]

    barrier = pltpu.get_barrier_semaphore()

    around = partners(sides, chip)
    for place_of in around[1:]:
        for side in (0, 1):
            pl.semaphore_signal(barrier, inc=1, device_id=(sec, place_of * 2 + side), device_id_type=MESH)
    pl.semaphore_signal(barrier, inc=1, device_id=(sec, chip * 2 + 1 - core), device_id_type=MESH)
    pl.semaphore_signal(barrier, inc=1, device_id=(prv, me), device_id_type=MESH)
    pl.semaphore_signal(barrier, inc=1, device_id=(mir, me), device_id_type=MESH)

    loads[3].wait()
    id0, id1 = ids[0:1, :], ids[1:2, :]
    kinds = iota((experts, tok), 0)
    one0, one1 = (id0 == kinds).astype(F32), (id1 == kinds).astype(F32)
    earlier = (iota((tok, tok), 0) < iota((tok, tok), 1)).astype(F32).astype(BF16)
    before = jnp.dot((one0 + one1).astype(BF16), earlier, preferred_element_type=F32)
    slot0 = jnp.sum(before * one0, axis=0, keepdims=True)
    slot1 = jnp.sum(before * one1, axis=0, keepdims=True)
    row0 = id0 * cap + slot0.astype(jnp.int32)
    row1 = id1 * cap + slot1.astype(jnp.int32)
    spots = iota((slots, tok), 0)
    place[...] = jnp.logical_or(spots == row0, spots == row1).astype(F32).astype(BF16)

    for load in loads[0:3]:
        load.wait()
    copy_wi.start()
    copy_wo.start()
    decoder = (sec >= sections // 2).astype(F32)
    block = 32

    def norm_rows(i, carry):
        at = pl.ds(pl.multiple_of(i * block, block), block)
        term = gain[...] * rms(skip[at, :].astype(F32))
        value = acts[at, :].astype(F32) + jnp.where(decoder > 0.5, term, jnp.zeros_like(term))
        h[at, :] = value
        normed[at, :] = rms(value).astype(BF16)
        return carry

    lax.fori_loop(0, tok // block, norm_rows, 0, unroll=2)

    in_width = width // IN_CHUNKS
    peers = 8

    def dispatch(c):
        def to_core(to):
            pltpu.make_async_remote_copy(
                src_ref=send.at[c, to], dst_ref=recv.at[core, c, chip],
                send_sem=in_send.at[c], recv_sem=in_recv.at[core, c],
                device_id=(sec, to), device_id_type=MESH,
            ).start()

        for place_of in around[1:]:
            to_core(place_of * 2 + 1 - core)
            to_core(place_of * 2 + core)
        to_core(chip * 2 + 1 - core)
        pltpu.make_async_copy(send.at[c, me], recv.at[core, c, chip], in_recv.at[core, c]).start()

    for c in range(IN_CHUNKS):
        def fill(i, carry, c=c):
            at = pl.ds(pl.multiple_of(i * peers * cap, peers * cap), peers * cap)
            got = jnp.dot(place[at, :], normed[:, c * in_width:(c + 1) * in_width], preferred_element_type=F32)
            send[c, pl.ds(i * peers, peers)] = got.reshape(peers, cap, in_width).astype(BF16)
            return carry

        lax.fori_loop(0, experts // peers, fill, 0)
        if c == 0:
            pl.semaphore_wait(barrier, experts + 1)

        @pl.when(first_core)
        def _(c=c):
            dispatch(c)

    loads[4].wait()
    logits = lax.dot_general(normed[...], router[...], (((1,), (1,)), ((), ())), preferred_element_type=F32)
    lines = iota((8, tok), 0)
    info = jnp.where(lines == 0, id0.astype(F32), jnp.where(lines == 1, id1.astype(F32), jnp.where(lines == 2, slot0, slot1)))
    eye = (iota((tok, tok), 0) == iota((tok, tok), 1)).astype(F32).astype(BF16)
    column = lax.dot_general(eye, info.astype(BF16), (((1,), (1,)), ((), ())), preferred_element_type=F32)
    names = iota((tok, experts), 1).astype(F32)
    chosen0 = jnp.sum(jnp.where(names == column[:, 0:1], logits, 0.0), axis=1, keepdims=True)
    chosen1 = jnp.sum(jnp.where(names == column[:, 1:2], logits, 0.0), axis=1, keepdims=True)
    top = jnp.maximum(chosen0, chosen1)
    exp0, exp1 = jnp.exp(chosen0 - top), jnp.exp(chosen1 - top)
    gate0, gate1 = exp0 / (exp0 + exp1), exp1 / (exp0 + exp1)
    spot0 = column[:, 0:1] * cap + column[:, 2:3]
    spot1 = column[:, 1:2] * cap + column[:, 3:4]
    along = iota((tok, slots), 1).astype(F32)
    gates = jnp.where(along == spot0, gate0, 0.0) + jnp.where(along == spot1, gate1, 0.0)
    high = gates.astype(BF16)
    mix[0:tok, :] = high
    mix[tok:, :] = (gates - high.astype(F32)).astype(BF16)

    copy_wi.wait()
    pair = 2
    tile = 256

    def enter(group):
        for c in range(IN_CHUNKS):
            pltpu.make_async_copy(recv.at[group, c], recv.at[group, c], in_recv.at[group, c]).wait()
            if group == 0 and c == IN_CHUNKS - 1:
                @pl.when(second_core)
                def _():
                    dispatch(0)

            span = pl.ds(c * in_width, in_width)

            def flatten(i, carry, c=c, span=span):
                at = pl.ds(pl.multiple_of(i * pair * cap, pair * cap), pair * cap)
                got = recv[group, c, pl.ds(i * pair, pair)].astype(F32)
                rows[at, span] = got.reshape(pair * cap, in_width).astype(BF16)
                return carry

            lax.fori_loop(0, chips // pair, flatten, 0)

            def first(n, carry, c=c, span=span):
                at = pl.ds(pl.multiple_of(n * tile, tile), tile)
                got = jnp.dot(rows[:, span], wi[span, at], preferred_element_type=F32)
                if c > 0:
                    got = acc[:, at] + got
                if c < IN_CHUNKS - 1:
                    acc[:, at] = got
                else:
                    hidden[:, at] = jax.nn.gelu(got, approximate=True).astype(BF16)
                return carry

            lax.fori_loop(0, ff // tile, first, 0)

    out_width = width // OUT_CHUNKS

    def leave(group, c):
        at = pl.ds(pl.multiple_of(c * out_width, out_width), out_width)
        got = jnp.dot(hidden[...], wo[:, at], preferred_element_type=F32)
        outs[group, c] = got.reshape(chips, cap, out_width).astype(BF16)

        def give_back(to):
            pltpu.make_async_remote_copy(
                src_ref=outs.at[group, c, to], dst_ref=back.at[c, me],
                send_sem=out_send.at[group, c], recv_sem=out_recv.at[c],
                device_id=(sec, to * 2 + group), device_id_type=MESH,
            ).start()

        for place_of in around[1:]:
            give_back(place_of)

        @pl.when(core == group)
        def _():
            pltpu.make_async_copy(outs.at[group, c, chip], back.at[c, me], out_recv.at[c]).start()

        @pl.when(core != group)
        def _():
            give_back(chip)

    def to_next(c):
        at = pl.ds(pl.multiple_of(c * out_width, out_width), out_width)
        return pltpu.make_async_remote_copy(
            src_ref=ys.at[c], dst_ref=handed.at[:, at],
            send_sem=z_send.at[0, c], recv_sem=z_recv.at[0, c],
            device_id=(nxt, me), device_id_type=MESH,
        )

    def to_mirror(c):
        at = pl.ds(pl.multiple_of(c * out_width, out_width), out_width)
        return pltpu.make_async_remote_copy(
            src_ref=ys.at[c], dst_ref=mirrored.at[:, at],
            send_sem=z_send.at[1, c], recv_sem=z_recv.at[1, c],
            device_id=(mir, me), device_id_type=MESH,
        )

    def double(c):
        at = pl.ds(pl.multiple_of(c * out_width, out_width), out_width)
        return pltpu.make_async_copy(handed.at[:, at], mirrored.at[:, at], dup_sem.at[c])

    sends_one = nxt == mir
    gets_one = prv == mir

    def combine(c, carry):
        pltpu.make_async_copy(back.at[c], back.at[c], out_recv.at[c]).wait()
        at = pl.ds(pl.multiple_of(c * out_width, out_width), out_width)
        got = back[c].astype(F32).reshape(slots, out_width).astype(BF16)
        both = jnp.dot(mix[...], got, preferred_element_type=F32)
        ys[c] = (h[:, at] + (both[0:tok] + both[tok:])).astype(BF16)
        to_next(c).start()

        @pl.when(jnp.logical_not(sends_one))
        def _():
            to_mirror(c).start()

        return carry

    enter(0)
    copy_wo.wait()

    def begin(j, carry):
        @pl.when(j < OUT_CHUNKS)
        def _():
            leave(0, j)

        for part, after in enumerate(AFTER):
            @pl.when(jnp.logical_and(second_core, j == after))
            def _(part=part):
                dispatch(part + 1)

        c = j - GAP

        @pl.when(jnp.logical_and(first_core, jnp.logical_and(c >= 0, c < EARLY)))
        def _():
            combine(c, 0)

        return carry

    lax.fori_loop(0, max(OUT_CHUNKS, EARLY + GAP), begin, 0)
    enter(1)

    def last(j, carry):
        @pl.when(j < OUT_CHUNKS)
        def _():
            leave(1, j)

        c = j + jnp.where(first_core, EARLY, -LEAD)

        @pl.when(jnp.logical_and(c >= 0, c < OUT_CHUNKS))
        def _():
            combine(c, 0)

        return carry

    lax.fori_loop(0, OUT_CHUNKS + LEAD, last, 0)

    def arrive(c, carry):
        to_next(c).wait_recv()

        @pl.when(gets_one)
        def _():
            double(c).start()

        @pl.when(jnp.logical_not(gets_one))
        def _():
            to_mirror(c).wait_recv()

        return carry

    lax.fori_loop(0, OUT_CHUNKS, arrive, 0)

    def sent(group, c, count):
        some = pl.ds(0, count)
        pltpu.make_async_copy(outs.at[group, c, some], outs.at[group, c, some], out_send.at[group, c]).wait()

    def finish(c, carry):
        @pl.when(gets_one)
        def _():
            double(c).wait()

        to_next(c).wait_send()

        @pl.when(jnp.logical_not(sends_one))
        def _():
            to_mirror(c).wait_send()

        @pl.when(first_core)
        def _():
            sent(0, c, chips - 1)
            sent(1, c, chips)

        @pl.when(second_core)
        def _():
            sent(0, c, chips)
            sent(1, c, chips - 1)

        return carry

    lax.fori_loop(0, OUT_CHUNKS, finish, 0)
    for c in range(IN_CHUNKS):
        others = pl.ds(0, experts - 1)
        pltpu.make_async_copy(send.at[c, others], send.at[c, others], in_send.at[c]).wait()


def store(first, second, first_out, second_out, sem):
    copies = [
        pltpu.make_async_copy(first, first_out, sem.at[0]),
        pltpu.make_async_copy(second, second_out, sem.at[1]),
    ]
    for copy in copies:
        copy.start()
    for copy in copies:
        copy.wait()


def local(sides, acts, expert_ids, router, skip_gain, skip_rows, w_in, w_out):
    sections = lax.axis_size("section")
    tok, width = acts.shape[1], acts.shape[2]
    experts = router.shape[2]
    topk = expert_ids.shape[2]
    cap = 3 * tok * topk // (2 * experts)
    ff = w_in.shape[3]
    slots = experts * cap
    in_width, out_width = width // IN_CHUNKS, width // OUT_CHUNKS
    vmem = pl.BlockSpec(memory_space=pltpu.VMEM)
    hbm = pl.BlockSpec(memory_space=pltpu.HBM)
    out = jax.ShapeDtypeStruct((tok, width), BF16)
    dma = pltpu.SemaphoreType.DMA
    handed, mirrored = pl.pallas_call(
        functools.partial(kernel, sides, sections, experts, cap),
        out_shape=(out, out),
        in_specs=[hbm] * 7,
        out_specs=(vmem, vmem),
        scratch_shapes=[
            pltpu.VMEM((tok, width), BF16),
            pltpu.VMEM((topk, tok), jnp.int32),
            pltpu.VMEM((experts, width), BF16),
            pltpu.VMEM((1, width), F32),
            pltpu.VMEM((tok, width), BF16),
            pltpu.VMEM((width, ff), BF16),
            pltpu.VMEM((ff, width), BF16),
            pltpu.VMEM((tok, width), F32),
            pltpu.VMEM((tok, width), BF16),
            pltpu.VMEM((slots, tok), BF16),
            pltpu.VMEM((2 * tok, slots), BF16),
            pltpu.VMEM((IN_CHUNKS, experts, cap, in_width), BF16),
            pltpu.VMEM((2, IN_CHUNKS, experts // 2, cap, in_width), BF16),
            pltpu.VMEM((slots // 2, width), BF16),
            pltpu.VMEM((slots // 2, ff), F32),
            pltpu.VMEM((slots // 2, ff), BF16),
            pltpu.VMEM((2, OUT_CHUNKS, experts // 2, cap, out_width), BF16),
            pltpu.VMEM((OUT_CHUNKS, experts, cap, out_width), BF16),
            pltpu.VMEM((OUT_CHUNKS, tok, out_width), BF16),
            dma((7,)),
            dma((IN_CHUNKS,)),
            dma((2, IN_CHUNKS)),
            dma((2, OUT_CHUNKS)),
            dma((OUT_CHUNKS,)),
            dma((2, OUT_CHUNKS)),
            dma((2, OUT_CHUNKS)),
            dma((OUT_CHUNKS,)),
        ],
        compiler_params=pltpu.CompilerParams(
            collective_id=0, has_side_effects=True, vmem_limit_bytes=44 * 1024 * 1024
        ),
        name="moe_window",
    )(*(
        pltpu.with_memory_space_constraint(value, pltpu.HBM)
        for value in (acts[0], expert_ids[0].T, router[0].T, skip_gain, skip_rows[0], w_in[0, 0], w_out[0, 0])
    ))
    handed, mirrored = pl.pallas_call(
        store,
        out_shape=(out, out),
        in_specs=[vmem, vmem],
        out_specs=(hbm, hbm),
        scratch_shapes=[dma((2,))],
        compiler_params=pltpu.CompilerParams(vmem_limit_bytes=8 * 1024 * 1024),
        name="store",
    )(handed, mirrored)
    return (handed[None], mirrored[None])


def solution(mesh):
    placed = (
        P("section", "expert", None),
        P("section", "expert", None),
        P("section", None, None),
        P("section", None),
        P("section", "expert", None),
        P("section", "expert", None, None),
        P("section", "expert", None, None),
    )
    return jax.shard_map(
        functools.partial(local, (4, 4)),
        mesh=mesh,
        in_specs=placed,
        out_specs=(P("section", "expert", None), P("section", "expert", None)),
        check_vma=False,
    )
```

```python
import functools

import jax
import jax.numpy as jnp
from jax import lax
from jax.experimental import pallas as pl
from jax.experimental.pallas import tpu as pltpu
from jax.sharding import PartitionSpec as P

MESH = pl.DeviceIdType.MESH
F32 = jnp.float32
BF16 = jnp.bfloat16

IN_CHUNKS = 4
OUT_CHUNKS = 8
EARLY = 7
AFTER = (1, 3, 6)
LEAD = 2
GAP = 2


def rms(values):
    return values * lax.rsqrt(jnp.mean(values * values, axis=-1, keepdims=True) + 1e-06)


def iota(shape, axis):
    return lax.broadcasted_iota(jnp.int32, shape, axis)


def partners(sides, chip):
    nx, ny = sides
    x, y = chip // ny, chip % ny
    columns = [(x + a) % nx * ny for a in range(nx)]
    lines = [(y + b) % ny for b in range(ny)]
    steps = [(a, (a + b) % ny) for b in range(ny) for a in range(nx)]
    reach = lambda step: min(step[0], nx - step[0]) + min(step[1], ny - step[1])
    return [columns[a] + lines[b] for a, b in steps[:1] + sorted(steps[1:], key=reach, reverse=True)]


def kernel(
    sides, sections, experts, cap,
    acts_in, ids_in, router_in, gain_in, skip_in, w_in, w_out,
    handed, mirrored,
    acts, ids, router, gain, skip, wi, wo, h, normed, place, mix, send, recv, rows, acc, hidden, outs, back, ys,
    w_sem, in_send, in_recv, out_send, out_recv, z_send, z_recv, dup_sem,
):
    sec = lax.axis_index("section")
    me = lax.axis_index("expert")
    core, chip = me % 2, me // 2
    chips = experts // 2
    first_core, second_core = core == 0, core == 1
    tok, width = acts.shape
    ff = w_in.shape[1]
    slots = experts * cap
    nxt, mir = (sec + 1) % sections, sections - 1 - sec
    prv = (sec + sections - 1) % sections

    loads = [
        pltpu.make_async_copy(source, target, w_sem.at[n])
        for n, (source, target) in enumerate((
            (acts_in, acts), (skip_in, skip), (gain_in, gain), (ids_in, ids),
            (router_in, router), (w_in, wi), (w_out, wo),
        ))
    ]
    for n in (3, 0, 1, 2, 4):
        loads[n].start()
    copy_wi, copy_wo = loads[5], loads[6]

    barrier = pltpu.get_barrier_semaphore()

    around = partners(sides, chip)
    for place_of in around[1:]:
        for side in (0, 1):
            pl.semaphore_signal(barrier, inc=1, device_id=(sec, place_of * 2 + side), device_id_type=MESH)
    pl.semaphore_signal(barrier, inc=1, device_id=(sec, chip * 2 + 1 - core), device_id_type=MESH)
    pl.semaphore_signal(barrier, inc=1, device_id=(prv, me), device_id_type=MESH)
    pl.semaphore_signal(barrier, inc=1, device_id=(mir, me), device_id_type=MESH)

    loads[3].wait()
    id0, id1 = ids[0:1, :], ids[1:2, :]
    kinds = iota((experts, tok), 0)
    one0, one1 = (id0 == kinds).astype(F32), (id1 == kinds).astype(F32)
    earlier = (iota((tok, tok), 0) < iota((tok, tok), 1)).astype(F32).astype(BF16)
    before = jnp.dot((one0 + one1).astype(BF16), earlier, preferred_element_type=F32)
    slot0 = jnp.sum(before * one0, axis=0, keepdims=True)
    slot1 = jnp.sum(before * one1, axis=0, keepdims=True)
    row0 = id0 * cap + slot0.astype(jnp.int32)
    row1 = id1 * cap + slot1.astype(jnp.int32)
    spots = iota((slots, tok), 0)
    place[...] = jnp.logical_or(spots == row0, spots == row1).astype(F32).astype(BF16)

    for load in loads[0:3]:
        load.wait()
    copy_wi.start()
    copy_wo.start()
    decoder = (sec >= sections // 2).astype(F32)
    block = 32

    def norm_rows(i, carry):
        at = pl.ds(pl.multiple_of(i * block, block), block)
        term = gain[...] * rms(skip[at, :].astype(F32))
        value = acts[at, :].astype(F32) + jnp.where(decoder > 0.5, term, jnp.zeros_like(term))
        h[at, :] = value
        normed[at, :] = rms(value).astype(BF16)
        return carry

    lax.fori_loop(0, tok // block, norm_rows, 0, unroll=4)

    in_width = width // IN_CHUNKS
    peers = 8

    def dispatch(c):
        def to_core(to):
            pltpu.make_async_remote_copy(
                src_ref=send.at[c, to], dst_ref=recv.at[core, c, chip],
                send_sem=in_send.at[c], recv_sem=in_recv.at[core, c],
                device_id=(sec, to), device_id_type=MESH,
            ).start()

        for place_of in around[1:]:
            to_core(place_of * 2 + 1 - core)
            to_core(place_of * 2 + core)
        to_core(chip * 2 + 1 - core)
        pltpu.make_async_copy(send.at[c, me], recv.at[core, c, chip], in_recv.at[core, c]).start()

    for c in range(IN_CHUNKS):
        def fill(i, carry, c=c):
            at = pl.ds(pl.multiple_of(i * peers * cap, peers * cap), peers * cap)
            got = jnp.dot(place[at, :], normed[:, c * in_width:(c + 1) * in_width], preferred_element_type=F32)
            send[c, pl.ds(i * peers, peers)] = got.reshape(peers, cap, in_width).astype(BF16)
            return carry

        lax.fori_loop(0, experts // peers, fill, 0)
        if c == 0:
            pl.semaphore_wait(barrier, experts + 1)

        @pl.when(first_core)
        def _(c=c):
            dispatch(c)

    loads[4].wait()
    logits = lax.dot_general(normed[...], router[...], (((1,), (1,)), ((), ())), preferred_element_type=F32)
    lines = iota((8, tok), 0)
    info = jnp.where(lines == 0, id0.astype(F32), jnp.where(lines == 1, id1.astype(F32), jnp.where(lines == 2, slot0, slot1)))
    eye = (iota((tok, tok), 0) == iota((tok, tok), 1)).astype(F32).astype(BF16)
    column = lax.dot_general(eye, info.astype(BF16), (((1,), (1,)), ((), ())), preferred_element_type=F32)
    names = iota((tok, experts), 1).astype(F32)
    chosen0 = jnp.sum(jnp.where(names == column[:, 0:1], logits, 0.0), axis=1, keepdims=True)
    chosen1 = jnp.sum(jnp.where(names == column[:, 1:2], logits, 0.0), axis=1, keepdims=True)
    top = jnp.maximum(chosen0, chosen1)
    exp0, exp1 = jnp.exp(chosen0 - top), jnp.exp(chosen1 - top)
    gate0, gate1 = exp0 / (exp0 + exp1), exp1 / (exp0 + exp1)
    spot0 = column[:, 0:1] * cap + column[:, 2:3]
    spot1 = column[:, 1:2] * cap + column[:, 3:4]
    along = iota((tok, slots), 1).astype(F32)
    gates = jnp.where(along == spot0, gate0, 0.0) + jnp.where(along == spot1, gate1, 0.0)
    high = gates.astype(BF16)
    mix[0:tok, :] = high
    mix[tok:, :] = (gates - high.astype(F32)).astype(BF16)

    copy_wi.wait()
    pair = 2
    tile = 256

    def enter(group):
        for c in range(IN_CHUNKS):
            pltpu.make_async_copy(recv.at[group, c], recv.at[group, c], in_recv.at[group, c]).wait()
            if group == 0 and c == IN_CHUNKS - 1:
                @pl.when(second_core)
                def _():
                    dispatch(0)

            span = pl.ds(c * in_width, in_width)

            def flatten(i, carry, c=c, span=span):
                at = pl.ds(pl.multiple_of(i * pair * cap, pair * cap), pair * cap)
                got = recv[group, c, pl.ds(i * pair, pair)].astype(F32)
                rows[at, span] = got.reshape(pair * cap, in_width).astype(BF16)
                return carry

            lax.fori_loop(0, chips // pair, flatten, 0)

            def first(n, carry, c=c, span=span):
                at = pl.ds(pl.multiple_of(n * tile, tile), tile)
                got = jnp.dot(rows[:, span], wi[span, at], preferred_element_type=F32)
                if c > 0:
                    got = acc[:, at] + got
                if c < IN_CHUNKS - 1:
                    acc[:, at] = got
                else:
                    hidden[:, at] = jax.nn.gelu(got, approximate=True).astype(BF16)
                return carry

            lax.fori_loop(0, ff // tile, first, 0)

    out_width = width // OUT_CHUNKS

    def leave(group, c):
        at = pl.ds(pl.multiple_of(c * out_width, out_width), out_width)
        got = jnp.dot(hidden[...], wo[:, at], preferred_element_type=F32)
        outs[group, c] = got.reshape(chips, cap, out_width).astype(BF16)

        def give_back(to):
            pltpu.make_async_remote_copy(
                src_ref=outs.at[group, c, to], dst_ref=back.at[c, me],
                send_sem=out_send.at[group, c], recv_sem=out_recv.at[c],
                device_id=(sec, to * 2 + group), device_id_type=MESH,
            ).start()

        for place_of in around[1:]:
            give_back(place_of)

        @pl.when(core == group)
        def _():
            pltpu.make_async_copy(outs.at[group, c, chip], back.at[c, me], out_recv.at[c]).start()

        @pl.when(core != group)
        def _():
            give_back(chip)

    def to_next(c):
        at = pl.ds(pl.multiple_of(c * out_width, out_width), out_width)
        return pltpu.make_async_remote_copy(
            src_ref=ys.at[c], dst_ref=handed.at[:, at],
            send_sem=z_send.at[0, c], recv_sem=z_recv.at[0, c],
            device_id=(nxt, me), device_id_type=MESH,
        )

    def to_mirror(c):
        at = pl.ds(pl.multiple_of(c * out_width, out_width), out_width)
        return pltpu.make_async_remote_copy(
            src_ref=ys.at[c], dst_ref=mirrored.at[:, at],
            send_sem=z_send.at[1, c], recv_sem=z_recv.at[1, c],
            device_id=(mir, me), device_id_type=MESH,
        )

    def double(c):
        at = pl.ds(pl.multiple_of(c * out_width, out_width), out_width)
        return pltpu.make_async_copy(handed.at[:, at], mirrored.at[:, at], dup_sem.at[c])

    sends_one = nxt == mir
    gets_one = prv == mir

    def combine(c, carry):
        pltpu.make_async_copy(back.at[c], back.at[c], out_recv.at[c]).wait()
        at = pl.ds(pl.multiple_of(c * out_width, out_width), out_width)
        got = back[c].astype(F32).reshape(slots, out_width).astype(BF16)
        both = jnp.dot(mix[...], got, preferred_element_type=F32)
        ys[c] = (h[:, at] + (both[0:tok] + both[tok:])).astype(BF16)
        to_next(c).start()

        @pl.when(jnp.logical_not(sends_one))
        def _():
            to_mirror(c).start()

        return carry

    enter(0)
    copy_wo.wait()

    def begin(j, carry):
        @pl.when(j < OUT_CHUNKS)
        def _():
            leave(0, j)

        for part, after in enumerate(AFTER):
            @pl.when(jnp.logical_and(second_core, j == after))
            def _(part=part):
                dispatch(part + 1)

        c = j - GAP

        @pl.when(jnp.logical_and(first_core, jnp.logical_and(c >= 0, c < EARLY)))
        def _():
            combine(c, 0)

        return carry

    lax.fori_loop(0, max(OUT_CHUNKS, EARLY + GAP), begin, 0)
    enter(1)

    def last(j, carry):
        @pl.when(j < OUT_CHUNKS)
        def _():
            leave(1, j)

        c = j + jnp.where(first_core, EARLY, -LEAD)

        @pl.when(jnp.logical_and(c >= 0, c < OUT_CHUNKS))
        def _():
            combine(c, 0)

        return carry

    lax.fori_loop(0, OUT_CHUNKS + LEAD, last, 0)

    def arrive(c, carry):
        to_next(c).wait_recv()

        @pl.when(gets_one)
        def _():
            double(c).start()

        @pl.when(jnp.logical_not(gets_one))
        def _():
            to_mirror(c).wait_recv()

        return carry

    lax.fori_loop(0, OUT_CHUNKS, arrive, 0)

    def sent(group, c, count):
        some = pl.ds(0, count)
        pltpu.make_async_copy(outs.at[group, c, some], outs.at[group, c, some], out_send.at[group, c]).wait()

    def finish(c, carry):
        @pl.when(gets_one)
        def _():
            double(c).wait()

        to_next(c).wait_send()

        @pl.when(jnp.logical_not(sends_one))
        def _():
            to_mirror(c).wait_send()

        @pl.when(first_core)
        def _():
            sent(0, c, chips - 1)
            sent(1, c, chips)

        @pl.when(second_core)
        def _():
            sent(0, c, chips)
            sent(1, c, chips - 1)

        return carry

    lax.fori_loop(0, OUT_CHUNKS, finish, 0)
    for c in range(IN_CHUNKS):
        others = pl.ds(0, experts - 1)
        pltpu.make_async_copy(send.at[c, others], send.at[c, others], in_send.at[c]).wait()


def store(first, second, first_out, second_out, sem):
    copies = [
        pltpu.make_async_copy(first, first_out, sem.at[0]),
        pltpu.make_async_copy(second, second_out, sem.at[1]),
    ]
    for copy in copies:
        copy.start()
    for copy in copies:
        copy.wait()


def local(sides, acts, expert_ids, router, skip_gain, skip_rows, w_in, w_out):
    sections = lax.axis_size("section")
    tok, width = acts.shape[1], acts.shape[2]
    experts = router.shape[2]
    topk = expert_ids.shape[2]
    cap = 3 * tok * topk // (2 * experts)
    ff = w_in.shape[3]
    slots = experts * cap
    in_width, out_width = width // IN_CHUNKS, width // OUT_CHUNKS
    vmem = pl.BlockSpec(memory_space=pltpu.VMEM)
    hbm = pl.BlockSpec(memory_space=pltpu.HBM)
    out = jax.ShapeDtypeStruct((tok, width), BF16)
    dma = pltpu.SemaphoreType.DMA
    handed, mirrored = pl.pallas_call(
        functools.partial(kernel, sides, sections, experts, cap),
        out_shape=(out, out),
        in_specs=[hbm] * 7,
        out_specs=(vmem, vmem),
        scratch_shapes=[
            pltpu.VMEM((tok, width), BF16),
            pltpu.VMEM((topk, tok), jnp.int32),
            pltpu.VMEM((experts, width), BF16),
            pltpu.VMEM((1, width), F32),
            pltpu.VMEM((tok, width), BF16),
            pltpu.VMEM((width, ff), BF16),
            pltpu.VMEM((ff, width), BF16),
            pltpu.VMEM((tok, width), F32),
            pltpu.VMEM((tok, width), BF16),
            pltpu.VMEM((slots, tok), BF16),
            pltpu.VMEM((2 * tok, slots), BF16),
            pltpu.VMEM((IN_CHUNKS, experts, cap, in_width), BF16),
            pltpu.VMEM((2, IN_CHUNKS, experts // 2, cap, in_width), BF16),
            pltpu.VMEM((slots // 2, width), BF16),
            pltpu.VMEM((slots // 2, ff), F32),
            pltpu.VMEM((slots // 2, ff), BF16),
            pltpu.VMEM((2, OUT_CHUNKS, experts // 2, cap, out_width), BF16),
            pltpu.VMEM((OUT_CHUNKS, experts, cap, out_width), BF16),
            pltpu.VMEM((OUT_CHUNKS, tok, out_width), BF16),
            dma((7,)),
            dma((IN_CHUNKS,)),
            dma((2, IN_CHUNKS)),
            dma((2, OUT_CHUNKS)),
            dma((OUT_CHUNKS,)),
            dma((2, OUT_CHUNKS)),
            dma((2, OUT_CHUNKS)),
            dma((OUT_CHUNKS,)),
        ],
        compiler_params=pltpu.CompilerParams(
            collective_id=0, has_side_effects=True, vmem_limit_bytes=44 * 1024 * 1024
        ),
        name="moe_window",
    )(*(
        pltpu.with_memory_space_constraint(value, pltpu.HBM)
        for value in (acts[0], expert_ids[0].T, router[0].T, skip_gain, skip_rows[0], w_in[0, 0], w_out[0, 0])
    ))
    handed, mirrored = pl.pallas_call(
        store,
        out_shape=(out, out),
        in_specs=[vmem, vmem],
        out_specs=(hbm, hbm),
        scratch_shapes=[dma((2,))],
        compiler_params=pltpu.CompilerParams(vmem_limit_bytes=8 * 1024 * 1024),
        name="store",
    )(handed, mirrored)
    return (handed[None], mirrored[None])


def solution(mesh):
    placed = (
        P("section", "expert", None),
        P("section", "expert", None),
        P("section", None, None),
        P("section", None),
        P("section", "expert", None),
        P("section", "expert", None, None),
        P("section", "expert", None, None),
    )
    return jax.shard_map(
        functools.partial(local, (4, 4)),
        mesh=mesh,
        in_specs=placed,
        out_specs=(P("section", "expert", None), P("section", "expert", None)),
        check_vma=False,
    )
```
